1024 devices in a mesh: lon: 64 (over y_lo, x, core), lat: 16 (over y_hi, z).
Axes of the slice: x: 8, y: 8 (y_hi: 2, y_lo: 4; y = y_hi * 4 + y_lo), z: 8, core: 2. Of those that a mesh axis runs over, the one named last changes fastest.
Arguments:
- record_values: bfloat16 [4096, 256, 2, 128], P('lon', 'lat'), may hold values from -6 to 6
- record_cell: int32 [4096, 256, 2], P('lon', 'lat'), may hold values from 0 to 287
- record_instrument: int32 [4096, 256, 2], P('lon', 'lat'), may hold values from 0 to 7
- block_counts: int32 [4096, 256], P('lon', 'lat'), may hold values from 0 to 2, as said below
- background: bfloat16 [192, 1536, 2, 192], P('lat', 'lon'), may hold values from -6 to 6
- input_weight: bfloat16 [128, 192], replicated, may hold values from -0.5 to 0.5
- instrument_table: bfloat16 [8, 192], replicated, may hold values from -4 to 4
- lift_weight: bfloat16 [192, 384], replicated, may hold values from -0.4375 to 0.4375
- first_gain: bfloat16 [192], replicated, may hold values from 0.5 to 1.5
- attn_weight: bfloat16 [192, 576], replicated
- mix_weight: bfloat16 [192, 192], replicated, may hold values from -0.4375 to 0.4375
- second_gain: bfloat16 [192], replicated, may hold values from 0.5 to 1.5
- up_weight: bfloat16 [192, 768], replicated, may hold values from -0.4375 to 0.4375
- down_weight: bfloat16 [768, 192], replicated, may hold values from -0.21875 to 0.21875
Outputs:
- result: bfloat16 [192, 1536, 2, 192], P('lat', 'lon')
The draws below stay inside these ranges and needn't reach their ends.
Inputs may be any that keep to these rules, and one draw needn't show every extreme that they name: `block_counts`: each block's count is at most 2; for some tiles every source fills all 2 slots.
All inputs are finite; a program needn't handle non-finite values.
Results may differ from the reference program's by a relative error of at most 0.017.
Values may be sent and summed in bfloat16 or wider, within the bound.
A program may use at most 32 MiB of HBM per device.

```python
import jax
import jax.numpy as jnp
from jax import lax

C = 192
HEADS = 6
MLPW = 768
F = 128
INSTR = 8
LEV = 2
WLAT = 6
WLON = 12
CLAT = 12
CLON = 24
CAP = 2
HD = 32
NLAT = 192
NLON = 1536
N_LON = 64
N_LAT = 16


def draw_block_counts(key, part):
    first, second, third, fourth = jax.random.split(key, 4)
    base = jax.random.randint(first, (N_LON * N_LON, N_LAT * N_LAT), 0, CAP + 1)
    dense = jax.random.randint(second, (N_LON, N_LAT), 0, 8) == 0
    pick_lon = jax.random.randint(third, (), 0, N_LON)
    pick_lat = jax.random.randint(fourth, (), 0, N_LAT)
    forced = (jnp.arange(N_LON)[:, None] == pick_lon) & (jnp.arange(N_LAT)[None, :] == pick_lat)
    dense_all = jnp.tile(dense | forced, (N_LON, N_LAT))
    return jnp.where(dense_all, CAP, base).astype(jnp.int32)


def draw_attn_weight(key, part):
    spread = C ** (-0.5)
    base = jax.random.normal(key, (C, 3 * C), jnp.float32) * spread
    return base.astype(jnp.bfloat16)


def place_ends(drawn, rng, smallest, high):
    place = [jax.random.randint(jax.random.fold_in(rng, axis), (), 0, length) for axis, length in enumerate(drawn.shape)]
    widest = drawn.shape.index(max(drawn.shape))
    neighbour = place[:widest] + [(place[widest] + 1) % drawn.shape[widest]] + place[widest + 1:]
    return drawn.at[tuple(place)].set(smallest).at[tuple(neighbour)].set(high)


def block_levels(own_key, shape, cuts, smallest, high):
    factor_of, own = 1.0, jax.random.fold_in(own_key, 6)
    for axis_at, blocks in cuts:
        steps = jnp.exp(jax.random.uniform(jax.random.fold_in(own, axis_at), (blocks,), jnp.float32, smallest / len(cuts), high / len(cuts)))
        factor_of = factor_of * jnp.repeat(steps, shape[axis_at] // blocks).reshape([-1 if axis == axis_at else 1 for axis in range(len(shape))])
    return factor_of


def normal_values(key, extent, deviation, reach, shards=(), held_as=jnp.bfloat16):
    level = block_levels(key, extent, shards, -0.22, 0.18) if shards else 1.0
    values = jax.random.normal(key, extent, jnp.float32) * deviation * level
    return jnp.minimum(jnp.maximum(values, -reach), reach).astype(held_as)


def setup_inputs(seed: int = 0) -> dict:
    streams_of = jax.random.split(jax.random.key(seed), 15)
    record_values = normal_values(streams_of[0], (N_LON * N_LON, N_LAT * N_LAT, CAP, F), 1.0, 6.0, ((0, 64), (1, 16)))
    record_cell = place_ends(jax.random.randint(streams_of[1], (N_LON * N_LON, N_LAT * N_LAT, CAP), 0, CLAT * CLON), jax.random.fold_in(streams_of[1], 1), 0, (CLAT * CLON) - 1).astype(jnp.int32)
    record_instrument = place_ends(jax.random.randint(streams_of[2], (N_LON * N_LON, N_LAT * N_LAT, CAP), 0, INSTR), jax.random.fold_in(streams_of[2], 1), 0, INSTR - 1).astype(jnp.int32)
    block_counts = draw_block_counts(jax.random.fold_in(streams_of[14], 71), 0)
    background = normal_values(streams_of[4], (NLAT, NLON, LEV, C), 1.0, 6.0, ((0, 16), (1, 64)))
    input_weight = normal_values(streams_of[5], (F, C), F ** -0.5, 0.5)
    instrument_table = normal_values(streams_of[6], (INSTR, C), 1.0, 4.0)
    lift_weight = normal_values(streams_of[7], (C, LEV * C), C ** -0.5, 0.4375)
    first_gain = jnp.clip(1.0 + 0.1 * jax.random.normal(streams_of[8], (C,), jnp.float32), 0.5, 1.5).astype(jnp.bfloat16)
    attn_weight = draw_attn_weight(jax.random.fold_in(streams_of[14], 71), 0)
    mix_weight = normal_values(streams_of[10], (C, C), C ** -0.5, 0.4375)
    second_gain = jnp.clip(1.0 + 0.1 * jax.random.normal(streams_of[11], (C,), jnp.float32), 0.5, 1.5).astype(jnp.bfloat16)
    up_weight = normal_values(streams_of[12], (C, MLPW), C ** -0.5, 0.4375)
    down_weight = normal_values(streams_of[13], (MLPW, C), MLPW ** -0.5, 0.21875)
    return {"record_values": record_values, "record_cell": record_cell, "record_instrument": record_instrument, "block_counts": block_counts, "background": background, "input_weight": input_weight, "instrument_table": instrument_table, "lift_weight": lift_weight, "first_gain": first_gain, "attn_weight": attn_weight, "mix_weight": mix_weight, "second_gain": second_gain, "up_weight": up_weight, "down_weight": down_weight}


def layer_norm(tensor, norm_gain):
    wide = tensor.astype(jnp.float32)
    average = lax.optimization_barrier(jnp.mean(wide, axis=-1, keepdims=True))
    centred = wide - average
    spread = lax.optimization_barrier(jnp.mean(centred * centred, axis=-1, keepdims=True))
    return (centred * lax.rsqrt(spread + 1e-05) * norm_gain.astype(jnp.float32)).astype(jnp.bfloat16)

def to_windows(tensor):
    height, breadth, levels, width = tensor.shape
    shaped = tensor.reshape(height // WLAT, WLAT, breadth // WLON, WLON, levels, width)
    shaped = shaped.transpose(0, 2, 1, 3, 4, 5)
    return shaped.reshape(height // WLAT * (breadth // WLON), WLAT * WLON * levels, width)

def from_windows(tensor, height, breadth):
    width = tensor.shape[-1]
    shaped = tensor.reshape(height // WLAT, breadth // WLON, WLAT, WLON, LEV, width)
    return shaped.transpose(0, 2, 1, 3, 4, 5).reshape(height, breadth, LEV, width)

def reference(record_values, record_cell, record_instrument, block_counts, background, input_weight, instrument_table, lift_weight, first_gain, attn_weight, mix_weight, second_gain, up_weight, down_weight):
    blocks = record_values.reshape(N_LON, N_LON, N_LAT, N_LAT, CAP, F)
    cell_blocks = record_cell.reshape(N_LON, N_LON, N_LAT, N_LAT, CAP)
    instr_blocks = record_instrument.reshape(N_LON, N_LON, N_LAT, N_LAT, CAP)
    count_blocks = block_counts.reshape(N_LON, N_LON, N_LAT, N_LAT)
    back_tiles = background.reshape(N_LAT, CLAT, N_LON, CLON, LEV, C)

    def tile_latent(tile_id):
        dest_lon = tile_id // N_LAT
        dest_lat = tile_id % N_LAT
        values = jnp.take(jnp.take(blocks, dest_lon, axis=1), dest_lat, axis=2).reshape(-1, F)
        cells = jnp.take(jnp.take(cell_blocks, dest_lon, axis=1), dest_lat, axis=2)
        instruments = jnp.take(jnp.take(instr_blocks, dest_lon, axis=1), dest_lat, axis=2).reshape(-1)
        counts = jnp.take(jnp.take(count_blocks, dest_lon, axis=1), dest_lat, axis=2)
        is_live = jnp.arange(CAP, dtype=jnp.int32)[None, None, :] < counts[:, :, None]
        before = jnp.dot(values, input_weight, preferred_element_type=jnp.float32)
        before = before + jnp.take(instrument_table, instruments, axis=0).astype(jnp.float32)
        encoded = jax.nn.gelu(before).astype(jnp.bfloat16)
        lifted = jax.nn.gelu(jnp.dot(encoded, lift_weight, preferred_element_type=jnp.float32)).astype(jnp.bfloat16)
        cell_flat = jnp.where(is_live, cells, -1).reshape(-1).astype(jnp.int32)
        onehot = (jnp.arange(CLAT * CLON, dtype=jnp.int32)[:, None] == cell_flat[None, :]).astype(jnp.bfloat16)
        summed = jnp.dot(onehot, lifted, preferred_element_type=jnp.float32)
        tallies = lax.optimization_barrier(jnp.sum(onehot.astype(jnp.float32), axis=1))
        prior = jnp.take(jnp.take(back_tiles, dest_lat, axis=0), dest_lon, axis=1).astype(jnp.float32)
        latent_tile = (prior + summed.reshape(CLAT, CLON, LEV, C)) / (1.0 + tallies).reshape(CLAT, CLON, 1, 1)
        return latent_tile.astype(jnp.bfloat16)
    tiles = lax.map(tile_latent, jnp.arange(N_LON * N_LAT, dtype=jnp.int32))
    latent = tiles.reshape(N_LON, N_LAT, CLAT, CLON, LEV, C).transpose(1, 2, 0, 3, 4, 5).reshape(NLAT, NLON, LEV, C)
    normed = layer_norm(latent, first_gain)
    rolled = jnp.roll(normed, (-(WLAT // 2), -(WLON // 2)), axis=(0, 1))
    projected = jnp.dot(rolled.reshape(-1, C), attn_weight, preferred_element_type=jnp.float32).reshape(NLAT, NLON, LEV, 3 * C)
    query = (projected[..., :C] * HD ** (-0.5)).astype(jnp.bfloat16)
    keys = projected[..., C:2 * C].astype(jnp.bfloat16)
    value_rows = projected[..., 2 * C:].astype(jnp.bfloat16)
    initial = (jnp.arange(NLAT, dtype=jnp.int32) + WLAT // 2) % NLAT
    region = (initial >= NLAT - WLAT // 2).astype(jnp.float32)
    region = jnp.broadcast_to(region[:, None, None, None], (NLAT, NLON, LEV, 1))
    row_windows = NLAT // WLAT
    col_windows = NLON // WLON
    tokens = WLAT * WLON * LEV
    query_w = to_windows(query).reshape(row_windows, col_windows, tokens, HEADS, HD)
    keys_w = to_windows(keys).reshape(row_windows, col_windows, tokens, HEADS, HD)
    values_w = to_windows(value_rows).reshape(row_windows, col_windows, tokens, HEADS, HD)
    region_w = to_windows(region).reshape(row_windows, col_windows, tokens)

    def window_row(pieces):
        query_p, keys_p, values_p, region_p = pieces
        scores = jnp.einsum('wqhd,wkhd->whqk', query_p.astype(jnp.float32), keys_p.astype(jnp.float32))
        allowed = region_p[:, None, :, None] == region_p[:, None, None, :]
        scores = jnp.where(allowed, scores, jnp.float32(-1e+30))
        largest = lax.optimization_barrier(jnp.max(scores, axis=-1, keepdims=True))
        raised = jnp.exp(scores - largest)
        attn_weights = (raised / lax.optimization_barrier(jnp.sum(raised, axis=-1, keepdims=True))).astype(jnp.bfloat16)
        out = jnp.einsum('whqk,wkhd->wqhd', attn_weights.astype(jnp.float32), values_p.astype(jnp.float32))
        return out.astype(jnp.bfloat16)
    mixed_w = lax.map(window_row, (query_w, keys_w, values_w, region_w))
    mixed_rolled = from_windows(mixed_w.reshape(row_windows * col_windows, tokens, C), NLAT, NLON)
    mixed = jnp.roll(mixed_rolled, (WLAT // 2, WLON // 2), axis=(0, 1))
    after_attn = latent.astype(jnp.float32) + jnp.dot(mixed.reshape(-1, C), mix_weight, preferred_element_type=jnp.float32).reshape(NLAT, NLON, LEV, C)
    after_attn = after_attn.astype(jnp.bfloat16)
    normed_two = layer_norm(after_attn, second_gain)
    hidden = jax.nn.gelu(jnp.dot(normed_two.reshape(-1, C), up_weight, preferred_element_type=jnp.float32)).astype(jnp.bfloat16)
    result = after_attn.astype(jnp.float32) + jnp.dot(hidden, down_weight, preferred_element_type=jnp.float32).reshape(NLAT, NLON, LEV, C)
    return result.astype(jnp.bfloat16)
```

```python
import functools

import jax
import jax.numpy as jnp
import numpy as np
from jax import lax
from jax.experimental import pallas as pl
from jax.experimental.pallas import tpu as pltpu
from jax.sharding import PartitionSpec as P

MESH = pl.DeviceIdType.MESH
HEADS = 6
INSTR = 8
LEV = 2
WLAT = 6
WLON = 12
FAR = -1e30

ROW_CUTS = (0, 3, 9, 12)
COL_CUTS = (0, 6, 18, 24)
ORDER = (("C", 1, 1), ("c00", 0, 0), ("T", 0, 1), ("c03", 0, 2), ("R", 1, 2), ("c33", 2, 2), ("B", 2, 1), ("c30", 2, 0), ("L", 1, 0))


def piece_table():
    table, cells = {}, 0
    for name, i, j in ORDER:
        count = (ROW_CUTS[i + 1] - ROW_CUTS[i]) * (COL_CUTS[j + 1] - COL_CUTS[j])
        padded = -(-count // 8) * 8
        table[name] = (cells, count, padded)
        cells += padded
    return table, cells


PIECES, CELLS = piece_table()
TOKENS = LEV * CELLS
HALO = 896
WIDE = 448


def base_of(i, j):
    name = [n for n, a, b in ORDER if (a, b) == (i, j)][0]
    return PIECES[name][0]


def cell_permutation():
    matrix = np.zeros((CELLS, 288), np.float32)
    for _, i, j in ORDER:
        breadth = COL_CUTS[j + 1] - COL_CUTS[j]
        for r in range(ROW_CUTS[i], ROW_CUTS[i + 1]):
            for c in range(COL_CUTS[j], COL_CUTS[j + 1]):
                place = base_of(i, j) + (r - ROW_CUTS[i]) * breadth + c - COL_CUTS[j]
                matrix[place, r * 24 + c] = 1.0
    return matrix


def dot_nn(a, b):
    return lax.dot_general(a, b, (((1,), (0,)), ((), ())), preferred_element_type=jnp.float32)


def dot_nt(a, b):
    return lax.dot_general(a, b, (((1,), (1,)), ((), ())), preferred_element_type=jnp.float32)


def dot_tn(a, b):
    return lax.dot_general(a, b, (((0,), (0,)), ((), ())), preferred_element_type=jnp.float32)


def norm(wide, gain):
    average = jnp.mean(wide, axis=-1, keepdims=True)
    centred = wide - average
    spread = jnp.mean(centred * centred, axis=-1, keepdims=True)
    return (centred * lax.rsqrt(spread + 1e-05) * gain).astype(jnp.bfloat16)


def gelu(x):
    return jax.nn.gelu(x, approximate=True)


def place_of(cell):
    row = jnp.floor((cell + 0.5) * (1.0 / 24.0))
    col = cell - 24.0 * row
    place = jnp.zeros_like(cell)
    for _, i, j in ORDER:
        breadth = COL_CUTS[j + 1] - COL_CUTS[j]
        inside = (row >= ROW_CUTS[i]) & (row < ROW_CUTS[i + 1]) & (col >= COL_CUTS[j]) & (col < COL_CUTS[j + 1])
        value = base_of(i, j) + (row - ROW_CUTS[i]) * breadth + (col - COL_CUTS[j])
        place = jnp.where(inside, value, place)
    return place


def kernel(
    n_lon,
    n_lat,
    values_hbm,
    cell_ref,
    instr_ref,
    count_ref,
    back_ref,
    perm_ref,
    win_ref,
    table_ref,
    lift_ref,
    gain1_ref,
    attn_ref,
    mix_ref,
    gain2_ref,
    up_ref,
    down_ref,
    out_ref,
    buf1,
    buf2,
    meta_s,
    meta_r,
    meta2_s,
    meta2_r,
    onehot_s,
    lifted_s,
    latent_s,
    normed_s,
    halo_s,
    q_s,
    k_s,
    v_s,
    kh_s,
    vh_s,
    mixed_s,
    back_s,
    own_sem,
    send1,
    sendm1,
    recv1,
    recvm1,
    send2,
    sendm2,
    recv2,
    recvm2,
    send3,
    recv3,
):
    lon = lax.axis_index("lon")
    lat = lax.axis_index("lat")
    lon_next, lon_prev = lax.rem(lon + 1, n_lon), lax.rem(lon + n_lon - 1, n_lon)
    lat_next, lat_prev = lax.rem(lat + 1, n_lat), lax.rem(lat + n_lat - 1, n_lat)
    slab = 2 * n_lon

    barrier = pltpu.get_barrier_semaphore()

    def greet_lon(k, _):
        pl.semaphore_signal(barrier, inc=1, device_id={"lon": lax.rem(lon + k, n_lon)}, device_id_type=MESH)
        return 0

    def greet_lat(k, _):
        pl.semaphore_signal(barrier, inc=1, device_id={"lat": lax.rem(lat + k, n_lat)}, device_id_type=MESH)
        return 0

    lax.fori_loop(1, n_lon, greet_lon, 0)
    lax.fori_loop(1, n_lat, greet_lat, 0)
    for a in (lat_prev, lat_next):
        for b in (lon_prev, lon_next):
            pl.semaphore_signal(barrier, inc=1, device_id={"lon": b, "lat": a}, device_id_type=MESH)

    count = count_ref[...]
    rows = [[], [], []]
    for slot in range(2):
        place = place_of(cell_ref[:, slot, :].astype(jnp.float32))
        high = jnp.floor(place * (1.0 / 16.0))
        rows[0].append(jnp.where(count > slot, high, -32.0))
        rows[1].append(place - 16.0 * high)
        rows[2].append(instr_ref[:, slot, :].astype(jnp.float32))
    stacked = jnp.concatenate(rows[0] + rows[1] + rows[2], axis=0).astype(jnp.bfloat16)
    wide_in = 6 * n_lat
    eye = (
        lax.broadcasted_iota(jnp.int32, (wide_in, 128), 0) == lax.broadcasted_iota(jnp.int32, (wide_in, 128), 1)
    ).astype(jnp.float32).astype(jnp.bfloat16)
    meta_s[:, 0, :] = dot_tn(stacked, eye)

    pl.semaphore_wait(barrier, n_lon - 1 + n_lat - 1 + 4)

    def send_lon(k, _):
        to = lax.rem(lon + k, n_lon)
        pltpu.make_async_remote_copy(
            src_ref=meta_s.at[to],
            dst_ref=meta_r.at[lon],
            send_sem=sendm1,
            recv_sem=recvm1,
            device_id={"lon": to},
            device_id_type=MESH,
        ).start()
        pltpu.make_async_remote_copy(
            src_ref=values_hbm.at[to],
            dst_ref=buf1.at[lon],
            send_sem=send1,
            recv_sem=recv1,
            device_id={"lon": to},
            device_id_type=MESH,
        ).start()
        return 0

    lax.fori_loop(1, n_lon, send_lon, 0)
    own1 = pltpu.make_async_copy(values_hbm.at[lon], buf1.at[lon], own_sem.at[0])
    own1.start()
    ownm1 = pltpu.make_async_copy(meta_s.at[lon], meta_r.at[lon], own_sem.at[1])
    ownm1.start()

    lifted_s[:, 384:512] = jnp.ones((n_lat * slab, 128), jnp.bfloat16)
    back_s[...] = dot_nn(perm_ref[...], back_ref[...])

    def wait_bytes(ref, sem):
        pltpu.make_async_copy(ref, ref, sem).wait()

    ownm1.wait()
    wait_bytes(meta_r.at[pl.ds(0, n_lon - 1)], recvm1)
    meta = meta_r[:, 0, :].astype(jnp.bfloat16)
    source = lax.broadcasted_iota(jnp.int32, (n_lon, slab), 0)
    lane = lax.broadcasted_iota(jnp.int32, (n_lon, slab), 1)
    slots = []
    for slot in range(2):
        spread = (lane == 2 * source + slot).astype(jnp.float32).astype(jnp.bfloat16)
        slots.append(dot_tn(meta, spread))
    for kind in range(3):
        first = kind * 2 * n_lat
        meta2_s[:, kind, 0:slab] = slots[0][first : first + n_lat] + slots[1][first + n_lat : first + 2 * n_lat]

    own1.wait()
    wait_bytes(buf1.at[pl.ds(0, n_lon - 1)], recv1)

    def send_lat(k, _):
        to = lax.rem(lat + k, n_lat)
        pltpu.make_async_remote_copy(
            src_ref=meta2_s.at[to],
            dst_ref=meta2_r.at[lat],
            send_sem=sendm2,
            recv_sem=recvm2.at[lat],
            device_id={"lat": to},
            device_id_type=MESH,
        ).start()
        pltpu.make_async_remote_copy(
            src_ref=buf1.at[:, to],
            dst_ref=buf2.at[lat],
            send_sem=send2,
            recv_sem=recv2.at[lat],
            device_id={"lat": to},
            device_id_type=MESH,
        ).start()
        return 0

    lax.fori_loop(1, n_lat, send_lat, 0)
    pltpu.make_async_copy(buf1.at[:, lat], buf2.at[lat], recv2.at[lat]).start()
    pltpu.make_async_copy(meta2_s.at[lat], meta2_r.at[lat], recvm2.at[lat]).start()

    def encode(k, _):
        came = lax.rem(lat + n_lat - k, n_lat)
        wait_bytes(meta2_r.at[came], recvm2.at[came])
        wait_bytes(buf2.at[came], recv2.at[came])
        info = meta2_r[came]
        info = info[:, 0:slab]
        place = info[0:1] * 16.0 + info[1:2]
        cells = lax.broadcasted_iota(jnp.int32, (CELLS, slab), 0).astype(jnp.float32)
        at = pl.multiple_of(k * slab, slab)
        onehot_s[:, pl.ds(at, slab)] = (cells == place).astype(jnp.float32).astype(jnp.bfloat16)
        tags = lax.broadcasted_iota(jnp.int32, (INSTR, slab), 0).astype(jnp.float32)
        chooser = (tags == info[2:3]).astype(jnp.float32).astype(jnp.bfloat16)
        records = buf2[came].reshape(slab, 128)
        before = dot_nt(records, win_ref[...]) + dot_tn(chooser, table_ref[...])
        encoded = gelu(before).astype(jnp.bfloat16)
        lifted = gelu(dot_nn(encoded, lift_ref[...])).astype(jnp.bfloat16)
        lifted_s[pl.ds(at, slab), 0:384] = lifted
        return 0

    lax.fori_loop(0, n_lat, encode, 0)

    total = dot_nn(onehot_s[...], lifted_s[...])
    tally = 1.0 + total[:, 384:385]
    mean = (back_s[...] + total[:, 0:384]) / tally
    parts = []
    for name, _, _ in ORDER:
        at, _, padded = PIECES[name]
        parts += [mean[at : at + padded, 0:192], mean[at : at + padded, 192:384]]
    latent = jnp.concatenate(parts, axis=0).astype(jnp.bfloat16)
    latent_s[...] = latent
    normed_s[...] = norm(latent.astype(jnp.float32), gain1_ref[...].astype(jnp.float32))

    def rows_of(name):
        at, _, padded = PIECES[name]
        return LEV * at, LEV * padded

    def span(first, last):
        a, _ = rows_of(first)
        b, size = rows_of(last)
        return a, b + size - a

    up_to = {"lat": lat_prev}
    down_to = {"lat": lat_next}
    sends = [
        (span("c00", "c03"), 0, up_to),
        (span("c03", "c33"), 176, {"lon": lon_next}),
        (span("c33", "c30"), 352, down_to),
        (span("c30", "L"), 528, {"lon": lon_prev}),
        (span("c00", "c00"), 656, {"lon": lon_prev}),
        (span("c00", "c00"), 704, {"lon": lon_prev, "lat": lat_prev}),
        (span("c03", "c03"), 752, {"lon": lon_next, "lat": lat_prev}),
        (span("c33", "c33"), 800, {"lon": lon_next, "lat": lat_next}),
        (span("c30", "c30"), 848, {"lon": lon_prev, "lat": lat_next}),
    ]
    copies = []
    for index, ((at, size), there, device) in enumerate(sends):
        copy = pltpu.make_async_remote_copy(
            src_ref=normed_s.at[pl.ds(at, size)],
            dst_ref=halo_s.at[pl.ds(there, size)],
            send_sem=send3.at[index],
            recv_sem=recv3.at[index],
            device_id=device,
            device_id_type=MESH,
        )
        copy.start()
        copies.append(copy)

    normed = normed_s[...]
    q_s[...] = (dot_nn(normed, attn_ref[:, 0:192]) * (32.0**-0.5)).astype(jnp.bfloat16)
    k_s[...] = dot_nn(normed, attn_ref[:, 192:384]).astype(jnp.bfloat16)
    v_s[...] = dot_nn(normed, attn_ref[:, 384:576]).astype(jnp.bfloat16)

    def heads_of(shape):
        return lax.broadcasted_iota(jnp.int32, shape, 1) // 32

    def attend(name, keys, values, bias):
        at, size = rows_of(name)
        query = q_s[pl.ds(at, size), :]
        head = heads_of((size, 192))
        stack = jnp.concatenate([jnp.where(head == h, query, jnp.zeros_like(query)) for h in range(HEADS)], axis=0)
        scores = dot_nt(stack, keys)
        if bias is not None:
            scores = scores + bias
        largest = jnp.max(scores, axis=-1, keepdims=True)
        raised = jnp.exp(scores - largest)
        weights = (raised / jnp.sum(raised, axis=-1, keepdims=True)).astype(jnp.bfloat16)
        output = dot_nn(weights, values)
        merged = output[0:size]
        for h in range(1, HEADS):
            merged = jnp.where(head == h, output[h * size : (h + 1) * size], merged)
        mixed_s[pl.ds(at, size), :] = merged.astype(jnp.bfloat16)

    at, size = rows_of("C")
    attend("C", k_s[pl.ds(at, size), :], v_s[pl.ds(at, size), :], None)

    for copy in copies:
        copy.wait_recv()
    halo = halo_s[...]
    kh_s[...] = dot_nn(halo, attn_ref[:, 192:384]).astype(jnp.bfloat16)
    vh_s[...] = dot_nn(halo, attn_ref[:, 384:576]).astype(jnp.bfloat16)

    windows = [
        ("T", [(400, 80)], lat == 0),
        ("B", [(48, 80)], lat == n_lat - 1),
        ("L", [(224, 80)], None),
        ("R", [(576, 80)], None),
        ("c00", [(176, 48), (480, 48), (800, 48)], lat == 0),
        ("c03", [(656, 48), (352, 48), (848, 48)], lat == 0),
        ("c30", [(304, 48), (0, 48), (752, 48)], lat == n_lat - 1),
        ("c33", [(528, 48), (128, 48), (704, 48)], lat == n_lat - 1),
    ]
    for name, others, edge in windows:
        at, size = rows_of(name)
        _, cells, padded = PIECES[name]
        count = size * (1 + len(others))
        keys = jnp.concatenate([k_s[pl.ds(at, size), :]] + [kh_s[pl.ds(a, n), :] for a, n in others], axis=0)
        values = jnp.concatenate([v_s[pl.ds(at, size), :]] + [vh_s[pl.ds(a, n), :] for a, n in others], axis=0)
        lane = lax.broadcasted_iota(jnp.int32, (1, count), 1)
        live = lax.rem(lane, padded) < cells
        if edge is not None:
            live = live & ((lane < count // 2) | jnp.logical_not(edge))
        attend(name, keys, values, jnp.where(live, 0.0, FAR))

    after = (latent_s[...].astype(jnp.float32) + dot_nn(mixed_s[...], mix_ref[...])).astype(jnp.bfloat16)
    after = after.astype(jnp.float32)
    normed_two = norm(after, gain2_ref[...].astype(jnp.float32))
    hidden = gelu(dot_nn(normed_two, up_ref[...])).astype(jnp.bfloat16)
    result = after + dot_nt(hidden, down_ref[...])
    for level in range(LEV):
        parts = []
        for name, _, _ in ORDER:
            at, size = rows_of(name)
            parts.append(result[at + level * (size // 2) : at + (level + 1) * (size // 2)])
        whole = jnp.concatenate(parts, axis=0).astype(jnp.bfloat16)
        out_ref[:, level * 192 : (level + 1) * 192] = dot_tn(perm_ref[...], whole).astype(jnp.bfloat16)

    wait_bytes(meta_s.at[pl.ds(0, n_lon - 1)], sendm1)
    wait_bytes(buf1.at[pl.ds(0, n_lon - 1)], send1)
    wait_bytes(meta2_s.at[pl.ds(0, n_lat - 1)], sendm2)
    wait_bytes(buf2.at[pl.ds(0, n_lat - 1)], send2)
    for copy in copies:
        copy.wait_send()


def local(
    n_lon,
    n_lat,
    record_values,
    record_cell,
    record_instrument,
    block_counts,
    background,
    input_weight,
    instrument_table,
    lift_weight,
    first_gain,
    attn_weight,
    mix_weight,
    second_gain,
    up_weight,
    down_weight,
):
    vmem = pl.BlockSpec(memory_space=pltpu.VMEM)
    perm = jnp.asarray(cell_permutation(), jnp.bfloat16)
    slab = 2 * n_lon
    out = pl.pallas_call(
        functools.partial(kernel, n_lon, n_lat),
        out_shape=jax.ShapeDtypeStruct((288, 384), jnp.bfloat16),
        in_specs=[pl.BlockSpec(memory_space=pl.ANY)] + [vmem] * 14,
        out_specs=vmem,
        scratch_shapes=[
            pltpu.VMEM((n_lon, n_lat, 2, 128), jnp.bfloat16),
            pltpu.VMEM((n_lat, n_lon, 2, 128), jnp.bfloat16),
            pltpu.VMEM((n_lon, 1, 128), jnp.float32),
            pltpu.VMEM((n_lon, 1, 128), jnp.float32),
            pltpu.VMEM((n_lat, 8, 128), jnp.float32),
            pltpu.VMEM((n_lat, 8, 128), jnp.float32),
            pltpu.VMEM((CELLS, n_lat * slab), jnp.bfloat16),
            pltpu.VMEM((n_lat * slab, 512), jnp.bfloat16),
            pltpu.VMEM((TOKENS, 192), jnp.bfloat16),
            pltpu.VMEM((TOKENS, 192), jnp.bfloat16),
            pltpu.VMEM((HALO, 192), jnp.bfloat16),
            pltpu.VMEM((TOKENS, 192), jnp.bfloat16),
            pltpu.VMEM((TOKENS, 192), jnp.bfloat16),
            pltpu.VMEM((TOKENS, 192), jnp.bfloat16),
            pltpu.VMEM((HALO, 192), jnp.bfloat16),
            pltpu.VMEM((HALO, 192), jnp.bfloat16),
            pltpu.VMEM((TOKENS, 192), jnp.bfloat16),
            pltpu.VMEM((CELLS, 384), jnp.float32),
            pltpu.SemaphoreType.DMA((2,)),
            pltpu.SemaphoreType.DMA,
            pltpu.SemaphoreType.DMA,
            pltpu.SemaphoreType.DMA,
            pltpu.SemaphoreType.DMA,
            pltpu.SemaphoreType.DMA,
            pltpu.SemaphoreType.DMA,
            pltpu.SemaphoreType.DMA((n_lat,)),
            pltpu.SemaphoreType.DMA((n_lat,)),
            pltpu.SemaphoreType.DMA((9,)),
            pltpu.SemaphoreType.DMA((9,)),
        ],
        compiler_params=pltpu.CompilerParams(
            collective_id=0, has_side_effects=True, vmem_limit_bytes=40 * 1024 * 1024
        ),
    )(
        record_values,
        record_cell.transpose(1, 2, 0),
        record_instrument.transpose(1, 2, 0),
        block_counts.transpose(1, 0),
        background.reshape(288, 384),
        perm,
        input_weight.T,
        instrument_table,
        lift_weight,
        first_gain.reshape(1, 192),
        attn_weight,
        mix_weight,
        second_gain.reshape(1, 192),
        up_weight,
        down_weight.T,
    )
    return out.reshape(12, 24, 2, 192)


def solution(mesh):
    placed = (
        P("lon", "lat", None, None),
        P("lon", "lat", None),
        P("lon", "lat", None),
        P("lon", "lat"),
        P("lat", "lon", None, None),
    ) + (P(),) * 9
    return jax.shard_map(
        functools.partial(local, mesh.shape["lon"], mesh.shape["lat"]),
        mesh=mesh,
        in_specs=placed,
        out_specs=P("lat", "lon", None, None),
        check_vma=False,
    )
```

```python
import functools

import jax
import jax.numpy as jnp
import numpy as np
from jax import lax
from jax.experimental import pallas as pl
from jax.experimental.pallas import tpu as pltpu
from jax.sharding import PartitionSpec as P

MESH = pl.DeviceIdType.MESH
HEADS = 6
INSTR = 8
LEV = 2
WLAT = 6
WLON = 12
FAR = -1e30

ROW_CUTS = (0, 3, 9, 12)
COL_CUTS = (0, 6, 18, 24)
ORDER = (("C", 1, 1), ("c00", 0, 0), ("T", 0, 1), ("c03", 0, 2), ("R", 1, 2), ("c33", 2, 2), ("B", 2, 1), ("c30", 2, 0), ("L", 1, 0))


def piece_table():
    table, cells = {}, 0
    for name, i, j in ORDER:
        count = (ROW_CUTS[i + 1] - ROW_CUTS[i]) * (COL_CUTS[j + 1] - COL_CUTS[j])
        padded = -(-count // 8) * 8
        table[name] = (cells, count, padded)
        cells += padded
    return table, cells


PIECES, CELLS = piece_table()
TOKENS = LEV * CELLS
HALO = 896


def base_of(i, j):
    name = [n for n, a, b in ORDER if (a, b) == (i, j)][0]
    return PIECES[name][0]


def dot_nn(a, b):
    return lax.dot_general(a, b, (((1,), (0,)), ((), ())), preferred_element_type=jnp.float32)


def dot_nt(a, b):
    return lax.dot_general(a, b, (((1,), (1,)), ((), ())), preferred_element_type=jnp.float32)


def dot_tn(a, b):
    return lax.dot_general(a, b, (((0,), (0,)), ((), ())), preferred_element_type=jnp.float32)


def norm(wide, gain):
    average = jnp.mean(wide, axis=-1, keepdims=True)
    centred = wide - average
    spread = jnp.mean(centred * centred, axis=-1, keepdims=True)
    return (centred * lax.rsqrt(spread + 1e-05) * gain).astype(jnp.bfloat16)


def gelu(x):
    return jax.nn.gelu(x, approximate=True)


def place_of(cell):
    row = jnp.floor((cell + 0.5) * (1.0 / 24.0))
    col = cell - 24.0 * row
    place = jnp.zeros_like(cell)
    for _, i, j in ORDER:
        breadth = COL_CUTS[j + 1] - COL_CUTS[j]
        inside = (row >= ROW_CUTS[i]) & (row < ROW_CUTS[i + 1]) & (col >= COL_CUTS[j]) & (col < COL_CUTS[j + 1])
        value = base_of(i, j) + (row - ROW_CUTS[i]) * breadth + (col - COL_CUTS[j])
        place = jnp.where(inside, value, place)
    return place


def token_of(source):
    cell = jnp.floor((source + 0.5) * 0.5)
    level = source - 2.0 * cell
    place = place_of(cell)
    token = jnp.zeros_like(source)
    for name, _, _ in ORDER:
        at, _, padded = PIECES[name]
        token = jnp.where(place >= at, place + at + level * padded, token)
    return token


def grid_of(n_lon, n_lat):
    n_yl, n_x = (4, 8) if n_lon == 64 else (2, 2)
    return n_yl, n_x, n_lon // (n_yl * n_x), 2, n_lat // 2


def kernel(
    n_lon,
    n_lat,
    values_hbm,
    cell_hbm,
    instr_hbm,
    count_hbm,
    back_hbm,
    win_hbm,
    table_hbm,
    lift_hbm,
    gain1_hbm,
    attn_hbm,
    mix_hbm,
    gain2_hbm,
    up_hbm,
    down_hbm,
    out_ref,
    cell_ref,
    instr_ref,
    count_ref,
    back_ref,
    win_ref,
    table_ref,
    lift_ref,
    gain1_ref,
    attn_ref,
    mix_ref,
    gain2_ref,
    up_ref,
    down_ref,
    perm_s,
    turn_s,
    load_sem,
    buf_a,
    buf_b,
    buf2,
    meta_s,
    meta_r,
    meta2_s,
    meta2_r,
    onehot_s,
    lifted_s,
    latent_s,
    normed_s,
    halo_s,
    q_s,
    k_s,
    v_s,
    kh_s,
    vh_s,
    mixed_s,
    back_s,
    own_sem,
    send_a,
    send_b,
    send_a2,
    send_b2,
    sendm1,
    recv_a,
    recv_b,
    recvm1,
    sendm2,
    recv2,
    recvm2,
    send3,
    recv3,
):
    lon = lax.axis_index("lon")
    lat = lax.axis_index("lat")
    lon_next, lon_prev = lax.rem(lon + 1, n_lon), lax.rem(lon + n_lon - 1, n_lon)
    lat_next, lat_prev = lax.rem(lat + 1, n_lat), lax.rem(lat + n_lat - 1, n_lat)
    slab = 2 * n_lon
    n_yl, n_x, n_c, n_yh, n_z = grid_of(n_lon, n_lat)
    core, x, yl = lax.rem(lon, n_c), lax.rem(lon // n_c, n_x), lon // (n_c * n_x)
    z, yh = lax.rem(lat, n_z), lat // n_z
    n_a, n_b = n_yh * n_yl * n_c, n_x * n_z

    def lon_of(a, b, c):
        return (a * n_x + b) * n_c + c

    def peer_a(k):
        i = lax.rem((yh * n_yl + yl) * n_c + core + k, n_a)
        to_c, to_yl, to_yh = lax.rem(i, n_c), lax.rem(i // n_c, n_yl), i // (n_c * n_yl)
        return to_yh, to_yl, to_c, {"lon": lon_of(to_yl, x, to_c), "lat": to_yh * n_z + z}

    def peer_b(k):
        i = lax.rem(x * n_z + z + k, n_b)
        to_z, to_x = lax.rem(i, n_z), i // n_z
        return to_x, to_z, {"lon": lon_of(yl, to_x, core), "lat": yh * n_z + to_z}

    barrier = pltpu.get_barrier_semaphore()

    def greet_lon(k, _):
        pl.semaphore_signal(barrier, inc=1, device_id={"lon": lax.rem(lon + k, n_lon)}, device_id_type=MESH)
        return 0

    def greet_lat(k, _):
        pl.semaphore_signal(barrier, inc=1, device_id={"lat": lax.rem(lat + k, n_lat)}, device_id_type=MESH)
        return 0

    def greet_a(k, _):
        pl.semaphore_signal(barrier, inc=1, device_id=peer_a(k)[-1], device_id_type=MESH)
        return 0

    def greet_b(k, _):
        pl.semaphore_signal(barrier, inc=1, device_id=peer_b(k)[-1], device_id_type=MESH)
        return 0

    lax.fori_loop(1, n_b, greet_b, 0)
    lax.fori_loop(1, n_a, greet_a, 0)
    lax.fori_loop(1, n_lon, greet_lon, 0)
    lax.fori_loop(1, n_lat, greet_lat, 0)
    for a in (lat_prev, lat_next):
        for b in (lon_prev, lon_next):
            pl.semaphore_signal(barrier, inc=1, device_id={"lon": b, "lat": a}, device_id_type=MESH)

    loads = []
    pairs = (
        (cell_hbm, cell_ref),
        (instr_hbm, instr_ref),
        (count_hbm, count_ref),
        (back_hbm, back_ref),
        (win_hbm, win_ref),
        (table_hbm, table_ref),
        (lift_hbm, lift_ref),
        (gain1_hbm, gain1_ref),
        (attn_hbm, attn_ref),
        (mix_hbm, mix_ref),
        (gain2_hbm, gain2_ref),
        (up_hbm, up_ref),
        (down_hbm, down_ref),
    )
    for index, (source, target) in enumerate(pairs):
        load = pltpu.make_async_copy(source, target, load_sem.at[index])
        load.start()
        loads.append(load)

    pl.semaphore_wait(barrier, n_a - 1 + n_b - 1 + n_lon - 1 + n_lat - 1 + 4)

    def send_lon(k, _):
        to = lax.rem(lon + k, n_lon)
        pltpu.make_async_remote_copy(
            src_ref=meta_s.at[to],
            dst_ref=meta_r.at[lon],
            send_sem=sendm1,
            recv_sem=recvm1,
            device_id={"lon": to},
            device_id_type=MESH,
        ).start()
        return 0

    def block_a(to_yh, to_yl, to_c):
        odd = lax.rem(to_yl, 2)
        return values_hbm.at[to_yl // 2, odd, :, odd, to_c, to_yh]

    def block_b(to_x, to_z):
        odd = lax.rem(to_x, 2)
        return values_hbm.at[:, 1 - odd, to_x // 2, odd, :, :, to_z]

    def send_first_a(k, _):
        to_yh, to_yl, to_c, device = peer_a(k)
        pltpu.make_async_remote_copy(
            src_ref=block_a(to_yh, to_yl, to_c),
            dst_ref=buf_a.at[yh, yl, core],
            send_sem=send_a.at[k],
            recv_sem=recv_a,
            device_id=device,
            device_id_type=MESH,
        ).start()
        return 0

    def send_first_b(k, _):
        to_x, to_z, device = peer_b(k)
        pltpu.make_async_remote_copy(
            src_ref=block_b(to_x, to_z),
            dst_ref=buf_b.at[z, x],
            send_sem=send_b.at[k],
            recv_sem=recv_b,
            device_id=device,
            device_id_type=MESH,
        ).start()
        return 0

    lax.fori_loop(1, n_a, send_first_a, 0)
    lax.fori_loop(1, n_b, send_first_b, 0)
    pltpu.make_async_copy(block_a(yh, yl, core), buf_a.at[yh, yl, core], recv_a).start()
    pltpu.make_async_copy(block_b(x, z), buf_b.at[z, x], recv_b).start()
    for load in loads[:3]:
        load.wait()
    count = count_ref[...]
    rows = [[], [], []]
    for slot in range(2):
        place = place_of(cell_ref[:, slot, :].astype(jnp.float32))
        high = jnp.floor(place * (1.0 / 16.0))
        rows[0].append(jnp.where(count > slot, high, -32.0))
        rows[1].append(place - 16.0 * high)
        rows[2].append(instr_ref[:, slot, :].astype(jnp.float32))
    stacked = jnp.concatenate(rows[0] + rows[1] + rows[2], axis=0).astype(jnp.bfloat16)
    wide_in = 6 * n_lat
    eye = (
        lax.broadcasted_iota(jnp.int32, (wide_in, 128), 0) == lax.broadcasted_iota(jnp.int32, (wide_in, 128), 1)
    ).astype(jnp.float32).astype(jnp.bfloat16)
    meta_s[:, 0, :] = dot_tn(stacked, eye)

    lax.fori_loop(1, n_lon, send_lon, 0)
    ownm1 = pltpu.make_async_copy(meta_s.at[lon], meta_r.at[lon], own_sem.at[1])
    ownm1.start()

    normed_s[...] = jnp.zeros_like(normed_s)
    lifted_s[:, 384:512] = jnp.ones((n_lat * slab, 128), jnp.bfloat16)
    token_row = token_of(lax.broadcasted_iota(jnp.int32, (1, 576), 1).astype(jnp.float32))
    token_at = lax.broadcasted_iota(jnp.int32, (TOKENS, 576), 0).astype(jnp.float32)
    perm_s[...] = (token_at == token_row).astype(jnp.float32).astype(jnp.bfloat16)
    token_col = token_of(lax.broadcasted_iota(jnp.int32, (576, 1), 0).astype(jnp.float32))
    token_on = lax.broadcasted_iota(jnp.int32, (576, TOKENS), 1).astype(jnp.float32)
    turn_s[...] = (token_on == token_col).astype(jnp.float32).astype(jnp.bfloat16)
    for load in loads[3:]:
        load.wait()
    back_s[...] = dot_nn(perm_s[...], back_ref[...].reshape(576, 192))

    def wait_bytes(ref, sem):
        pltpu.make_async_copy(ref, ref, sem).wait()

    odd_x, odd_y = lax.rem(x, 2), lax.rem(yl, 2)
    half_x, half_y = n_x // 2, n_yl // 2
    n_a2, n_b2 = half_y * n_yh * n_c, half_x * n_z
    mine_a = (yh * half_y + yl // 2) * n_c + core
    mine_b = (x // 2) * n_z + z

    def second_b(k):
        i = lax.rem(mine_b + k, n_b2)
        half, to_z = i // n_z, lax.rem(i, n_z)
        device = {"lon": lon_of(yl, 2 * half + odd_y, core), "lat": yh * n_z + to_z}
        return buf_a.at[:, :, :, half, to_z], buf2.at[:, z, :, x], device

    def second_a(k):
        i = lax.rem(mine_a + k, n_a2)
        to_c, half, to_yh = lax.rem(i, n_c), lax.rem(i // n_c, half_y), i // (n_c * half_y)
        device = {"lon": lon_of(2 * half + 1 - odd_x, x, to_c), "lat": to_yh * n_z + z}
        return buf_b.at[:, :, half, to_c, to_yh], buf2.at[yh, :, yl, :, core], device

    def send_second(part, sem):
        def send(k, _):
            source, target, device = part(k)
            pltpu.make_async_remote_copy(
                src_ref=source,
                dst_ref=target,
                send_sem=sem.at[k],
                recv_sem=recv2,
                device_id=device,
                device_id_type=MESH,
            ).start()
            return 0

        return send

    even = odd_x == odd_y

    wait_bytes(buf_b, recv_b)

    @pl.when(even)
    def _():
        send_second(second_a, send_a2)(0, 0)

    @pl.when(jnp.logical_not(even))
    def _():
        source, target, _ = second_a(0)
        pltpu.make_async_copy(source, target, recv2).start()

    lax.fori_loop(1, n_a2, send_second(second_a, send_a2), 0)
    wait_bytes(buf_a, recv_a)

    @pl.when(jnp.logical_not(even))
    def _():
        send_second(second_b, send_b2)(0, 0)

    @pl.when(even)
    def _():
        source, target, _ = second_b(0)
        pltpu.make_async_copy(source, target, recv2).start()

    lax.fori_loop(1, n_b2, send_second(second_b, send_b2), 0)
    ownm1.wait()
    wait_bytes(meta_r.at[pl.ds(0, n_lon - 1)], recvm1)
    meta = meta_r[:, 0, :].astype(jnp.bfloat16)
    source = lax.broadcasted_iota(jnp.int32, (n_lon, slab), 0)
    lane = lax.broadcasted_iota(jnp.int32, (n_lon, slab), 1)
    slots = []
    for slot in range(2):
        spread = (lane == 2 * source + slot).astype(jnp.float32).astype(jnp.bfloat16)
        slots.append(dot_tn(meta, spread))
    for kind in range(3):
        first = kind * 2 * n_lat
        meta2_s[:, kind, 0:slab] = slots[0][first : first + n_lat] + slots[1][first + n_lat : first + 2 * n_lat]


    def send_lat(k, _):
        to = lax.rem(lat + k, n_lat)
        pltpu.make_async_remote_copy(
            src_ref=meta2_s.at[to],
            dst_ref=meta2_r.at[lat],
            send_sem=sendm2,
            recv_sem=recvm2.at[lat],
            device_id={"lat": to},
            device_id_type=MESH,
        ).start()
        return 0

    lax.fori_loop(1, n_lat, send_lat, 0)
    pltpu.make_async_copy(meta2_s.at[lat], meta2_r.at[lat], recvm2.at[lat]).start()

    for came in range(n_lat):
        wait_bytes(meta2_r.at[came], recvm2.at[came])
    wait_bytes(buf2, recv2)

    def encode(k, _):
        info = meta2_r[k]
        info = info[:, 0:slab]
        place = info[0:1] * 16.0 + info[1:2]
        cells = lax.broadcasted_iota(jnp.int32, (CELLS, slab), 0).astype(jnp.float32)
        at = pl.multiple_of(k * slab, slab)
        onehot_s[:, pl.ds(at, slab)] = (cells == place).astype(jnp.float32).astype(jnp.bfloat16)
        tags = lax.broadcasted_iota(jnp.int32, (INSTR, slab), 0).astype(jnp.float32)
        chooser = (tags == info[2:3]).astype(jnp.float32).astype(jnp.bfloat16)
        records = buf2[k // n_z, lax.rem(k, n_z)].reshape(slab, 128)
        before = dot_nt(records, win_ref[...]) + dot_tn(chooser, table_ref[...])
        encoded = gelu(before).astype(jnp.bfloat16)
        lifted = gelu(dot_nn(encoded, lift_ref[...])).astype(jnp.bfloat16)
        lifted_s[pl.ds(at, slab), 0:384] = lifted
        return 0

    lax.fori_loop(0, n_lat, encode, 0)

    total = dot_nn(onehot_s[...], lifted_s[...])
    tally = 1.0 + total[:, 384:385]
    parts, tallies = [], []
    for name, _, _ in ORDER:
        at, _, padded = PIECES[name]
        parts += [total[at : at + padded, 0:192], total[at : at + padded, 192:384]]
        tallies += [tally[at : at + padded]] * 2
    latent = (back_s[...] + jnp.concatenate(parts, axis=0)) / jnp.concatenate(tallies, axis=0)
    latent = latent.astype(jnp.bfloat16)
    latent_s[...] = latent
    normed_s[:, 0:192] = norm(latent.astype(jnp.float32), gain1_ref[...].reshape(1, 192).astype(jnp.float32))

    def rows_of(name):
        at, _, padded = PIECES[name]
        return LEV * at, LEV * padded

    def span(first, last):
        a, _ = rows_of(first)
        b, size = rows_of(last)
        return a, b + size - a

    up_to = {"lat": lat_prev}
    down_to = {"lat": lat_next}
    sends = [
        (span("c00", "c03"), 0, up_to),
        (span("c03", "c33"), 176, {"lon": lon_next}),
        (span("c33", "c30"), 352, down_to),
        (span("c30", "L"), 528, {"lon": lon_prev}),
        (span("c00", "c00"), 656, {"lon": lon_prev}),
        (span("c00", "c00"), 704, {"lon": lon_prev, "lat": lat_prev}),
        (span("c03", "c03"), 752, {"lon": lon_next, "lat": lat_prev}),
        (span("c33", "c33"), 800, {"lon": lon_next, "lat": lat_next}),
        (span("c30", "c30"), 848, {"lon": lon_prev, "lat": lat_next}),
    ]
    copies = []
    for index, ((at, size), there, device) in enumerate(sends):
        copy = pltpu.make_async_remote_copy(
            src_ref=normed_s.at[pl.ds(at, size)],
            dst_ref=halo_s.at[pl.ds(there, size)],
            send_sem=send3.at[index],
            recv_sem=recv3.at[index],
            device_id=device,
            device_id_type=MESH,
        )
        copy.start()
        copies.append(copy)

    normed = normed_s[:, 0:192]
    q_s[...] = (dot_nn(normed, attn_ref[:, 0:192]) * (32.0**-0.5)).astype(jnp.bfloat16)
    k_s[...] = dot_nn(normed, attn_ref[:, 192:384]).astype(jnp.bfloat16)
    v_s[...] = dot_nn(normed, attn_ref[:, 384:576]).astype(jnp.bfloat16)

    def heads_of(shape):
        return lax.broadcasted_iota(jnp.int32, shape, 1) // 32

    def attend(name, keys, values, bias):
        at, size = rows_of(name)
        query = q_s[pl.ds(at, size), :]
        head = heads_of((size, 192))
        stack = jnp.concatenate([jnp.where(head == h, query, jnp.zeros_like(query)) for h in range(HEADS)], axis=0)
        scores = dot_nt(stack, keys)
        if bias is not None:
            scores = scores + bias
        largest = jnp.max(scores, axis=-1, keepdims=True)
        raised = jnp.exp(scores - largest)
        weights = (raised / jnp.sum(raised, axis=-1, keepdims=True)).astype(jnp.bfloat16)
        output = dot_nn(weights, values)
        merged = output[0:size]
        for h in range(1, HEADS):
            merged = jnp.where(head == h, output[h * size : (h + 1) * size], merged)
        mixed_s[pl.ds(at, size), :] = merged.astype(jnp.bfloat16)

    at, size = rows_of("C")
    attend("C", k_s[pl.ds(at, size), :], v_s[pl.ds(at, size), :], None)

    for copy in copies:
        copy.wait_recv()
    halo = halo_s[:, 0:192]
    kh_s[...] = dot_nn(halo, attn_ref[:, 192:384]).astype(jnp.bfloat16)
    vh_s[...] = dot_nn(halo, attn_ref[:, 384:576]).astype(jnp.bfloat16)

    windows = [
        ("T", [(400, 80)], lat == 0),
        ("B", [(48, 80)], lat == n_lat - 1),
        ("L", [(224, 80)], None),
        ("R", [(576, 80)], None),
        ("c00", [(176, 48), (480, 48), (800, 48)], lat == 0),
        ("c03", [(656, 48), (352, 48), (848, 48)], lat == 0),
        ("c30", [(304, 48), (0, 48), (752, 48)], lat == n_lat - 1),
        ("c33", [(528, 48), (128, 48), (704, 48)], lat == n_lat - 1),
    ]
    for name, others, edge in windows:
        at, size = rows_of(name)
        _, cells, padded = PIECES[name]
        count = size * (1 + len(others))
        keys = jnp.concatenate([k_s[pl.ds(at, size), :]] + [kh_s[pl.ds(a, n), :] for a, n in others], axis=0)
        values = jnp.concatenate([v_s[pl.ds(at, size), :]] + [vh_s[pl.ds(a, n), :] for a, n in others], axis=0)
        lane = lax.broadcasted_iota(jnp.int32, (1, count), 1)
        live = lax.rem(lane, padded) < cells
        if edge is not None:
            live = live & ((lane < count // 2) | jnp.logical_not(edge))
        attend(name, keys, values, jnp.where(live, 0.0, FAR))

    after = (latent_s[...].astype(jnp.float32) + dot_nn(mixed_s[...], mix_ref[...])).astype(jnp.bfloat16)
    after = after.astype(jnp.float32)
    normed_two = norm(after, gain2_ref[...].reshape(1, 192).astype(jnp.float32))
    hidden = gelu(dot_nn(normed_two, up_ref[...])).astype(jnp.bfloat16)
    result = after + dot_nt(hidden, down_ref[...])
    out_ref[...] = dot_nn(turn_s[...], result.astype(jnp.bfloat16)).astype(jnp.bfloat16)

    wait_bytes(meta_s.at[pl.ds(0, n_lon - 1)], sendm1)
    wait_bytes(meta2_s.at[pl.ds(0, n_lat - 1)], sendm2)

    def done_first_a(k, _):
        wait_bytes(buf_a.at[0, 0, 0], send_a.at[k])
        return 0

    def done_first_b(k, _):
        wait_bytes(buf_b.at[0, 0], send_b.at[k])
        return 0

    def done_second_a(k, _):
        wait_bytes(buf2.at[0, :, 0, :, 0], send_a2.at[k])
        return 0

    def done_second_b(k, _):
        wait_bytes(buf2.at[:, 0, :, 0], send_b2.at[k])
        return 0

    lax.fori_loop(1, n_a, done_first_a, 0)
    lax.fori_loop(1, n_b, done_first_b, 0)
    lax.fori_loop(1, n_a2, done_second_a, 0)
    lax.fori_loop(1, n_b2, done_second_b, 0)

    @pl.when(even)
    def _():
        done_second_a(0, 0)

    @pl.when(jnp.logical_not(even))
    def _():
        done_second_b(0, 0)

    for copy in copies:
        copy.wait_send()


def local(
    n_lon,
    n_lat,
    record_values,
    record_cell,
    record_instrument,
    block_counts,
    background,
    input_weight,
    instrument_table,
    lift_weight,
    first_gain,
    attn_weight,
    mix_weight,
    second_gain,
    up_weight,
    down_weight,
):
    vmem = pl.BlockSpec(memory_space=pltpu.VMEM)
    slab = 2 * n_lon
    n_yl, n_x, n_c, n_yh, n_z = grid_of(n_lon, n_lat)
    out = pl.pallas_call(
        functools.partial(kernel, n_lon, n_lat),
        out_shape=jax.ShapeDtypeStruct((576, 192), jnp.bfloat16),
        in_specs=[pl.BlockSpec(memory_space=pltpu.HBM)] * 14,
        out_specs=vmem,
        scratch_shapes=[
            pltpu.VMEM((n_lat, 2, n_lon), jnp.int32),
            pltpu.VMEM((n_lat, 2, n_lon), jnp.int32),
            pltpu.VMEM((n_lat, n_lon), jnp.int32),
            pltpu.VMEM((288, 2, 192), jnp.bfloat16),
            pltpu.VMEM((192, 128), jnp.bfloat16),
            pltpu.VMEM((INSTR, 192), jnp.bfloat16),
            pltpu.VMEM((192, 384), jnp.bfloat16),
            pltpu.VMEM((192,), jnp.bfloat16),
            pltpu.VMEM((192, 576), jnp.bfloat16),
            pltpu.VMEM((192, 192), jnp.bfloat16),
            pltpu.VMEM((192,), jnp.bfloat16),
            pltpu.VMEM((192, 768), jnp.bfloat16),
            pltpu.VMEM((192, 768), jnp.bfloat16),
            pltpu.VMEM((TOKENS, 576), jnp.bfloat16),
            pltpu.VMEM((576, TOKENS), jnp.bfloat16),
            pltpu.SemaphoreType.DMA((13,)),
            pltpu.VMEM((n_yh, n_yl, n_c, n_x // 2, n_z, 2, 128), jnp.bfloat16),
            pltpu.VMEM((n_z, n_x, n_yl // 2, n_c, n_yh, 2, 128), jnp.bfloat16),
            pltpu.VMEM((n_yh, n_z, n_yl, n_x, n_c, 2, 128), jnp.bfloat16),
            pltpu.VMEM((n_lon, 1, 128), jnp.float32),
            pltpu.VMEM((n_lon, 1, 128), jnp.float32),
            pltpu.VMEM((n_lat, 8, 128), jnp.float32),
            pltpu.VMEM((n_lat, 8, 128), jnp.float32),
            pltpu.VMEM((CELLS, n_lat * slab), jnp.bfloat16),
            pltpu.VMEM((n_lat * slab, 512), jnp.bfloat16),
            pltpu.VMEM((TOKENS, 192), jnp.bfloat16),
            pltpu.VMEM((TOKENS, 256), jnp.bfloat16),
            pltpu.VMEM((HALO, 256), jnp.bfloat16),
            pltpu.VMEM((TOKENS, 192), jnp.bfloat16),
            pltpu.VMEM((TOKENS, 192), jnp.bfloat16),
            pltpu.VMEM((TOKENS, 192), jnp.bfloat16),
            pltpu.VMEM((HALO, 192), jnp.bfloat16),
            pltpu.VMEM((HALO, 192), jnp.bfloat16),
            pltpu.VMEM((TOKENS, 192), jnp.bfloat16),
            pltpu.VMEM((TOKENS, 192), jnp.float32),
            pltpu.SemaphoreType.DMA((2,)),
            pltpu.SemaphoreType.DMA((n_yh * n_yl * n_c,)),
            pltpu.SemaphoreType.DMA((n_x * n_z,)),
            pltpu.SemaphoreType.DMA((n_yh * n_yl * n_c // 2,)),
            pltpu.SemaphoreType.DMA((n_x * n_z // 2,)),
            pltpu.SemaphoreType.DMA,
            pltpu.SemaphoreType.DMA,
            pltpu.SemaphoreType.DMA,
            pltpu.SemaphoreType.DMA,
            pltpu.SemaphoreType.DMA,
            pltpu.SemaphoreType.DMA,
            pltpu.SemaphoreType.DMA((n_lat,)),
            pltpu.SemaphoreType.DMA((9,)),
            pltpu.SemaphoreType.DMA((9,)),
        ],
        compiler_params=pltpu.CompilerParams(
            collective_id=0, has_side_effects=True, vmem_limit_bytes=40 * 1024 * 1024
        ),
    )(
        record_values.reshape(n_yl // 2, 2, n_x // 2, 2, n_c, n_yh, n_z, 2, 128),
        record_cell.transpose(1, 2, 0),
        record_instrument.transpose(1, 2, 0),
        block_counts.transpose(1, 0),
        background.reshape(288, 2, 192),
        input_weight.T,
        instrument_table,
        lift_weight,
        first_gain,
        attn_weight,
        mix_weight,
        second_gain,
        up_weight,
        down_weight.T,
    )
    return out.reshape(12, 24, 2, 192)


def solution(mesh):
    placed = (
        P("lon", "lat", None, None),
        P("lon", "lat", None),
        P("lon", "lat", None),
        P("lon", "lat"),
        P("lat", "lon", None, None),
    ) + (P(),) * 9
    return jax.shard_map(
        functools.partial(local, mesh.shape["lon"], mesh.shape["lat"]),
        mesh=mesh,
        in_specs=placed,
        out_specs=P("lat", "lon", None, None),
        check_vma=False,
    )
```

```python
import functools

import jax
import jax.numpy as jnp
import numpy as np
from jax import lax
from jax.experimental import pallas as pl
from jax.experimental.pallas import tpu as pltpu
from jax.sharding import PartitionSpec as P

MESH = pl.DeviceIdType.MESH
HEADS = 6
INSTR = 8
LEV = 2
WLAT = 6
WLON = 12
FAR = -1e30

ROW_CUTS = (0, 3, 9, 12)
COL_CUTS = (0, 6, 18, 24)
ORDER = (("C", 1, 1), ("c00", 0, 0), ("T", 0, 1), ("c03", 0, 2), ("R", 1, 2), ("c33", 2, 2), ("B", 2, 1), ("c30", 2, 0), ("L", 1, 0))


def piece_table():
    table, cells = {}, 0
    for name, i, j in ORDER:
        count = (ROW_CUTS[i + 1] - ROW_CUTS[i]) * (COL_CUTS[j + 1] - COL_CUTS[j])
        padded = -(-count // 8) * 8
        table[name] = (cells, count, padded)
        cells += padded
    return table, cells


PIECES, CELLS = piece_table()
TOKENS = LEV * CELLS
HALO = 896


def base_of(i, j):
    name = [n for n, a, b in ORDER if (a, b) == (i, j)][0]
    return PIECES[name][0]


def dot_nn(a, b):
    return lax.dot_general(a, b, (((1,), (0,)), ((), ())), preferred_element_type=jnp.float32)


def dot_nt(a, b):
    return lax.dot_general(a, b, (((1,), (1,)), ((), ())), preferred_element_type=jnp.float32)


def dot_tn(a, b):
    return lax.dot_general(a, b, (((0,), (0,)), ((), ())), preferred_element_type=jnp.float32)


def norm(wide, gain):
    average = jnp.mean(wide, axis=-1, keepdims=True)
    centred = wide - average
    spread = jnp.mean(centred * centred, axis=-1, keepdims=True)
    return (centred * lax.rsqrt(spread + 1e-05) * gain).astype(jnp.bfloat16)


def gelu(x):
    return jax.nn.gelu(x, approximate=True)


def place_of(cell):
    row = jnp.floor((cell + 0.5) * (1.0 / 24.0))
    col = cell - 24.0 * row
    place = jnp.zeros_like(cell)
    for _, i, j in ORDER:
        breadth = COL_CUTS[j + 1] - COL_CUTS[j]
        inside = (row >= ROW_CUTS[i]) & (row < ROW_CUTS[i + 1]) & (col >= COL_CUTS[j]) & (col < COL_CUTS[j + 1])
        value = base_of(i, j) + (row - ROW_CUTS[i]) * breadth + (col - COL_CUTS[j])
        place = jnp.where(inside, value, place)
    return place


def token_of(source):
    cell = jnp.floor((source + 0.5) * 0.5)
    level = source - 2.0 * cell
    place = place_of(cell)
    token = jnp.zeros_like(source)
    for name, _, _ in ORDER:
        at, _, padded = PIECES[name]
        token = jnp.where(place >= at, place + at + level * padded, token)
    return token


def grid_of(n_lon, n_lat):
    n_yl, n_x = (4, 8) if n_lon == 64 else (2, 2)
    return n_yl, n_x, n_lon // (n_yl * n_x), 2, n_lat // 2


def kernel(
    n_lon,
    n_lat,
    values_hbm,
    cell_hbm,
    instr_hbm,
    count_hbm,
    back_hbm,
    win_hbm,
    table_hbm,
    lift_hbm,
    gain1_hbm,
    attn_hbm,
    mix_hbm,
    gain2_hbm,
    up_hbm,
    down_hbm,
    out_ref,
    cell_ref,
    instr_ref,
    count_ref,
    back_ref,
    win_ref,
    table_ref,
    lift_ref,
    gain1_ref,
    attn_ref,
    mix_ref,
    gain2_ref,
    up_ref,
    down_ref,
    perm_s,
    turn_s,
    load_sem,
    buf_a,
    buf_b,
    buf2,
    meta_s,
    meta_r,
    meta2_s,
    meta2_r,
    onehot_s,
    lifted_s,
    latent_s,
    normed_s,
    halo_s,
    q_s,
    k_s,
    v_s,
    kh_s,
    vh_s,
    mixed_s,
    back_s,
    own_sem,
    send_a,
    send_b,
    send_a2,
    send_b2,
    sendm1,
    recv_a,
    recv_b,
    recvm1,
    sendm2,
    recv2,
    recvm2,
    send3,
    recv3,
):
    lon = lax.axis_index("lon")
    lat = lax.axis_index("lat")
    lon_next, lon_prev = lax.rem(lon + 1, n_lon), lax.rem(lon + n_lon - 1, n_lon)
    lat_next, lat_prev = lax.rem(lat + 1, n_lat), lax.rem(lat + n_lat - 1, n_lat)
    slab = 2 * n_lon
    n_yl, n_x, n_c, n_yh, n_z = grid_of(n_lon, n_lat)
    core, x, yl = lax.rem(lon, n_c), lax.rem(lon // n_c, n_x), lon // (n_c * n_x)
    z, yh = lax.rem(lat, n_z), lat // n_z
    n_a, n_b = n_yh * n_yl * n_c, n_x * n_z

    def lon_of(a, b, c):
        return (a * n_x + b) * n_c + c

    def peer_a(k):
        i = lax.rem((yh * n_yl + yl) * n_c + core + k, n_a)
        to_c, to_yl, to_yh = lax.rem(i, n_c), lax.rem(i // n_c, n_yl), i // (n_c * n_yl)
        return to_yh, to_yl, to_c, {"lon": lon_of(to_yl, x, to_c), "lat": to_yh * n_z + z}

    def peer_b(k):
        i = lax.rem(x * n_z + z + k, n_b)
        to_z, to_x = lax.rem(i, n_z), i // n_z
        return to_x, to_z, {"lon": lon_of(yl, to_x, core), "lat": yh * n_z + to_z}

    barrier = pltpu.get_barrier_semaphore()

    def greet_lon(k, _):
        pl.semaphore_signal(barrier, inc=1, device_id={"lon": lax.rem(lon + k, n_lon)}, device_id_type=MESH)
        return 0

    def greet_lat(k, _):
        pl.semaphore_signal(barrier, inc=1, device_id={"lat": lax.rem(lat + k, n_lat)}, device_id_type=MESH)
        return 0

    def greet_a(k, _):
        pl.semaphore_signal(barrier, inc=1, device_id=peer_a(k)[-1], device_id_type=MESH)
        return 0

    def greet_b(k, _):
        pl.semaphore_signal(barrier, inc=1, device_id=peer_b(k)[-1], device_id_type=MESH)
        return 0

    lax.fori_loop(1, n_b, greet_b, 0)
    lax.fori_loop(1, n_a, greet_a, 0)
    lax.fori_loop(1, n_lon, greet_lon, 0)
    lax.fori_loop(1, n_lat, greet_lat, 0)
    for a in (lat_prev, lat_next):
        for b in (lon_prev, lon_next):
            pl.semaphore_signal(barrier, inc=1, device_id={"lon": b, "lat": a}, device_id_type=MESH)

    loads = []
    pairs = (
        (cell_hbm, cell_ref),
        (instr_hbm, instr_ref),
        (count_hbm, count_ref),
        (back_hbm, back_ref),
        (win_hbm, win_ref),
        (table_hbm, table_ref),
        (lift_hbm, lift_ref),
        (gain1_hbm, gain1_ref),
        (attn_hbm, attn_ref),
        (mix_hbm, mix_ref),
        (gain2_hbm, gain2_ref),
        (up_hbm, up_ref),
        (down_hbm, down_ref),
    )
    for index, (source, target) in enumerate(pairs):
        load = pltpu.make_async_copy(source, target, load_sem.at[index])
        load.start()
        loads.append(load)

    pl.semaphore_wait(barrier, n_a - 1 + n_b - 1 + n_lon - 1 + n_lat - 1 + 4)

    def send_lon(k, _):
        to = lax.rem(lon + k, n_lon)
        pltpu.make_async_remote_copy(
            src_ref=meta_s.at[to],
            dst_ref=meta_r.at[lon],
            send_sem=sendm1,
            recv_sem=recvm1,
            device_id={"lon": to},
            device_id_type=MESH,
        ).start()
        return 0

    def block_a(to_yh, to_yl, to_c):
        odd = lax.rem(to_yl, 2)
        return values_hbm.at[to_yl // 2, odd, :, odd, to_c, to_yh]

    def block_b(to_x, to_z):
        odd = lax.rem(to_x, 2)
        return values_hbm.at[:, 1 - odd, to_x // 2, odd, :, :, to_z]

    def send_first_a(k, _):
        to_yh, to_yl, to_c, device = peer_a(k)
        pltpu.make_async_remote_copy(
            src_ref=block_a(to_yh, to_yl, to_c),
            dst_ref=buf_a.at[yh, yl, core],
            send_sem=send_a.at[k],
            recv_sem=recv_a,
            device_id=device,
            device_id_type=MESH,
        ).start()
        return 0

    def send_first_b(k, _):
        to_x, to_z, device = peer_b(k)
        pltpu.make_async_remote_copy(
            src_ref=block_b(to_x, to_z),
            dst_ref=buf_b.at[z, x],
            send_sem=send_b.at[k],
            recv_sem=recv_b,
            device_id=device,
            device_id_type=MESH,
        ).start()
        return 0

    lax.fori_loop(1, n_a, send_first_a, 0)
    lax.fori_loop(1, n_b, send_first_b, 0)
    pltpu.make_async_copy(block_a(yh, yl, core), buf_a.at[yh, yl, core], recv_a).start()
    pltpu.make_async_copy(block_b(x, z), buf_b.at[z, x], recv_b).start()
    for load in loads[:3]:
        load.wait()
    count = count_ref[...]
    rows = [[], [], []]
    for slot in range(2):
        place = place_of(cell_ref[:, slot, :].astype(jnp.float32))
        high = jnp.floor(place * (1.0 / 16.0))
        rows[0].append(jnp.where(count > slot, high, -32.0))
        rows[1].append(place - 16.0 * high)
        rows[2].append(instr_ref[:, slot, :].astype(jnp.float32))
    stacked = jnp.concatenate(rows[0] + rows[1] + rows[2], axis=0).astype(jnp.bfloat16)
    wide_in = 6 * n_lat
    eye = (
        lax.broadcasted_iota(jnp.int32, (wide_in, 128), 0) == lax.broadcasted_iota(jnp.int32, (wide_in, 128), 1)
    ).astype(jnp.float32).astype(jnp.bfloat16)
    meta_s[:, 0, :] = dot_tn(stacked, eye)

    lax.fori_loop(1, n_lon, send_lon, 0)
    ownm1 = pltpu.make_async_copy(meta_s.at[lon], meta_r.at[lon], own_sem.at[1])
    ownm1.start()

    normed_s[...] = jnp.zeros_like(normed_s)
    lifted_s[:, 384:512] = jnp.ones((n_lat * slab, 128), jnp.bfloat16)
    token_row = token_of(lax.broadcasted_iota(jnp.int32, (1, 576), 1).astype(jnp.float32))
    token_at = lax.broadcasted_iota(jnp.int32, (TOKENS, 576), 0).astype(jnp.float32)
    perm_s[...] = (token_at == token_row).astype(jnp.float32).astype(jnp.bfloat16)
    token_col = token_of(lax.broadcasted_iota(jnp.int32, (576, 1), 0).astype(jnp.float32))
    token_on = lax.broadcasted_iota(jnp.int32, (576, TOKENS), 1).astype(jnp.float32)
    turn_s[...] = (token_on == token_col).astype(jnp.float32).astype(jnp.bfloat16)
    for load in loads[3:]:
        load.wait()
    back_s[...] = dot_nn(perm_s[...], back_ref[...].reshape(576, 192))

    def wait_bytes(ref, sem):
        pltpu.make_async_copy(ref, ref, sem).wait()

    odd_x, odd_y = lax.rem(x, 2), lax.rem(yl, 2)
    half_x, half_y = n_x // 2, n_yl // 2
    n_a2, n_b2 = half_y * n_yh * n_c, half_x * n_z
    mine_a = (yh * half_y + yl // 2) * n_c + core
    mine_b = (x // 2) * n_z + z

    def second_b(k):
        i = lax.rem(mine_b + k, n_b2)
        half, to_z = i // n_z, lax.rem(i, n_z)
        device = {"lon": lon_of(yl, 2 * half + odd_y, core), "lat": yh * n_z + to_z}
        return buf_a.at[:, :, :, half, to_z], buf2.at[:, z, :, x], device

    def second_a(k):
        i = lax.rem(mine_a + k, n_a2)
        to_c, half, to_yh = lax.rem(i, n_c), lax.rem(i // n_c, half_y), i // (n_c * half_y)
        device = {"lon": lon_of(2 * half + 1 - odd_x, x, to_c), "lat": to_yh * n_z + z}
        return buf_b.at[:, :, half, to_c, to_yh], buf2.at[yh, :, yl, :, core], device

    def send_second(part, sem):
        def send(k, _):
            source, target, device = part(k)
            pltpu.make_async_remote_copy(
                src_ref=source,
                dst_ref=target,
                send_sem=sem.at[k],
                recv_sem=recv2,
                device_id=device,
                device_id_type=MESH,
            ).start()
            return 0

        return send

    even = odd_x == odd_y

    wait_bytes(buf_b, recv_b)

    @pl.when(even)
    def _():
        send_second(second_a, send_a2)(0, 0)

    @pl.when(jnp.logical_not(even))
    def _():
        source, target, _ = second_a(0)
        pltpu.make_async_copy(source, target, recv2).start()

    lax.fori_loop(1, n_a2, send_second(second_a, send_a2), 0)
    wait_bytes(buf_a, recv_a)

    @pl.when(jnp.logical_not(even))
    def _():
        send_second(second_b, send_b2)(0, 0)

    @pl.when(even)
    def _():
        source, target, _ = second_b(0)
        pltpu.make_async_copy(source, target, recv2).start()

    lax.fori_loop(1, n_b2, send_second(second_b, send_b2), 0)
    ownm1.wait()
    wait_bytes(meta_r.at[pl.ds(0, n_lon - 1)], recvm1)
    meta = meta_r[:, 0, :].astype(jnp.bfloat16)
    source = lax.broadcasted_iota(jnp.int32, (n_lon, slab), 0)
    lane = lax.broadcasted_iota(jnp.int32, (n_lon, slab), 1)
    slots = []
    for slot in range(2):
        spread = (lane == 2 * source + slot).astype(jnp.float32).astype(jnp.bfloat16)
        slots.append(dot_tn(meta, spread))
    for kind in range(3):
        first = kind * 2 * n_lat
        meta2_s[:, kind, 0:slab] = slots[0][first : first + n_lat] + slots[1][first + n_lat : first + 2 * n_lat]


    def send_lat(k, _):
        to = lax.rem(lat + k, n_lat)
        pltpu.make_async_remote_copy(
            src_ref=meta2_s.at[to],
            dst_ref=meta2_r.at[lat],
            send_sem=sendm2,
            recv_sem=recvm2.at[lat],
            device_id={"lat": to},
            device_id_type=MESH,
        ).start()
        return 0

    lax.fori_loop(1, n_lat, send_lat, 0)
    pltpu.make_async_copy(meta2_s.at[lat], meta2_r.at[lat], recvm2.at[lat]).start()

    for came in range(n_lat):
        wait_bytes(meta2_r.at[came], recvm2.at[came])
    wait_bytes(buf2, recv2)

    def encode(k, _):
        info = meta2_r[k]
        info = info[:, 0:slab]
        place = info[0:1] * 16.0 + info[1:2]
        cells = lax.broadcasted_iota(jnp.int32, (CELLS, slab), 0).astype(jnp.float32)
        at = pl.multiple_of(k * slab, slab)
        onehot_s[:, pl.ds(at, slab)] = (cells == place).astype(jnp.float32).astype(jnp.bfloat16)
        tags = lax.broadcasted_iota(jnp.int32, (INSTR, slab), 0).astype(jnp.float32)
        chooser = (tags == info[2:3]).astype(jnp.float32).astype(jnp.bfloat16)
        records = buf2[k // n_z, lax.rem(k, n_z)].reshape(slab, 128)
        before = dot_nt(records, win_ref[...]) + dot_tn(chooser, table_ref[...])
        encoded = gelu(before).astype(jnp.bfloat16)
        lifted = gelu(dot_nn(encoded, lift_ref[...])).astype(jnp.bfloat16)
        lifted_s[pl.ds(at, slab), 0:384] = lifted
        return 0

    lax.fori_loop(0, n_lat, encode, 0, unroll=2)

    total = dot_nn(onehot_s[...], lifted_s[...])
    tally = 1.0 + total[:, 384:385]
    parts, tallies = [], []
    for name, _, _ in ORDER:
        at, _, padded = PIECES[name]
        parts += [total[at : at + padded, 0:192], total[at : at + padded, 192:384]]
        tallies += [tally[at : at + padded]] * 2
    latent = (back_s[...] + jnp.concatenate(parts, axis=0)) / jnp.concatenate(tallies, axis=0)
    latent = latent.astype(jnp.bfloat16)
    latent_s[...] = latent
    normed_s[:, 0:192] = norm(latent.astype(jnp.float32), gain1_ref[...].reshape(1, 192).astype(jnp.float32))

    def rows_of(name):
        at, _, padded = PIECES[name]
        return LEV * at, LEV * padded

    def span(first, last):
        a, _ = rows_of(first)
        b, size = rows_of(last)
        return a, b + size - a

    up_to = {"lat": lat_prev}
    down_to = {"lat": lat_next}
    sends = [
        (span("c00", "c03"), 0, up_to),
        (span("c03", "c33"), 176, {"lon": lon_next}),
        (span("c33", "c30"), 352, down_to),
        (span("c30", "L"), 528, {"lon": lon_prev}),
        (span("c00", "c00"), 656, {"lon": lon_prev}),
        (span("c00", "c00"), 704, {"lon": lon_prev, "lat": lat_prev}),
        (span("c03", "c03"), 752, {"lon": lon_next, "lat": lat_prev}),
        (span("c33", "c33"), 800, {"lon": lon_next, "lat": lat_next}),
        (span("c30", "c30"), 848, {"lon": lon_prev, "lat": lat_next}),
    ]
    copies = []
    for index, ((at, size), there, device) in enumerate(sends):
        copy = pltpu.make_async_remote_copy(
            src_ref=normed_s.at[pl.ds(at, size)],
            dst_ref=halo_s.at[pl.ds(there, size)],
            send_sem=send3.at[index],
            recv_sem=recv3.at[index],
            device_id=device,
            device_id_type=MESH,
        )
        copy.start()
        copies.append(copy)

    normed = normed_s[:, 0:192]
    q_s[...] = (dot_nn(normed, attn_ref[:, 0:192]) * (32.0**-0.5)).astype(jnp.bfloat16)
    k_s[...] = dot_nn(normed, attn_ref[:, 192:384]).astype(jnp.bfloat16)
    v_s[...] = dot_nn(normed, attn_ref[:, 384:576]).astype(jnp.bfloat16)

    def heads_of(shape):
        return lax.broadcasted_iota(jnp.int32, shape, 1) // 32

    def attend(name, keys, values, bias):
        at, size = rows_of(name)
        query = q_s[pl.ds(at, size), :]
        head = heads_of((size, 192))
        stack = jnp.concatenate([jnp.where(head == h, query, jnp.zeros_like(query)) for h in range(HEADS)], axis=0)
        scores = dot_nt(stack, keys)
        if bias is not None:
            scores = scores + bias
        largest = jnp.max(scores, axis=-1, keepdims=True)
        raised = jnp.exp(scores - largest)
        weights = (raised / jnp.sum(raised, axis=-1, keepdims=True)).astype(jnp.bfloat16)
        output = dot_nn(weights, values)
        merged = output[0:size]
        for h in range(1, HEADS):
            merged = jnp.where(head == h, output[h * size : (h + 1) * size], merged)
        mixed_s[pl.ds(at, size), :] = merged.astype(jnp.bfloat16)

    at, size = rows_of("C")
    attend("C", k_s[pl.ds(at, size), :], v_s[pl.ds(at, size), :], None)

    for copy in copies:
        copy.wait_recv()
    halo = halo_s[:, 0:192]
    kh_s[...] = dot_nn(halo, attn_ref[:, 192:384]).astype(jnp.bfloat16)
    vh_s[...] = dot_nn(halo, attn_ref[:, 384:576]).astype(jnp.bfloat16)

    windows = [
        ("T", [(400, 80)], lat == 0),
        ("B", [(48, 80)], lat == n_lat - 1),
        ("L", [(224, 80)], None),
        ("R", [(576, 80)], None),
        ("c00", [(176, 48), (480, 48), (800, 48)], lat == 0),
        ("c03", [(656, 48), (352, 48), (848, 48)], lat == 0),
        ("c30", [(304, 48), (0, 48), (752, 48)], lat == n_lat - 1),
        ("c33", [(528, 48), (128, 48), (704, 48)], lat == n_lat - 1),
    ]
    for name, others, edge in windows:
        at, size = rows_of(name)
        _, cells, padded = PIECES[name]
        count = size * (1 + len(others))
        keys = jnp.concatenate([k_s[pl.ds(at, size), :]] + [kh_s[pl.ds(a, n), :] for a, n in others], axis=0)
        values = jnp.concatenate([v_s[pl.ds(at, size), :]] + [vh_s[pl.ds(a, n), :] for a, n in others], axis=0)
        lane = lax.broadcasted_iota(jnp.int32, (1, count), 1)
        live = lax.rem(lane, padded) < cells
        if edge is not None:
            live = live & ((lane < count // 2) | jnp.logical_not(edge))
        attend(name, keys, values, jnp.where(live, 0.0, FAR))

    after = (latent_s[...].astype(jnp.float32) + dot_nn(mixed_s[...], mix_ref[...])).astype(jnp.bfloat16)
    after = after.astype(jnp.float32)
    normed_two = norm(after, gain2_ref[...].reshape(1, 192).astype(jnp.float32))
    hidden = gelu(dot_nn(normed_two, up_ref[...])).astype(jnp.bfloat16)
    result = after + dot_nt(hidden, down_ref[...])
    out_ref[...] = dot_nn(turn_s[...], result.astype(jnp.bfloat16)).astype(jnp.bfloat16)

    wait_bytes(meta_s.at[pl.ds(0, n_lon - 1)], sendm1)
    wait_bytes(meta2_s.at[pl.ds(0, n_lat - 1)], sendm2)

    def done_first_a(k, _):
        wait_bytes(buf_a.at[0, 0, 0], send_a.at[k])
        return 0

    def done_first_b(k, _):
        wait_bytes(buf_b.at[0, 0], send_b.at[k])
        return 0

    def done_second_a(k, _):
        wait_bytes(buf2.at[0, :, 0, :, 0], send_a2.at[k])
        return 0

    def done_second_b(k, _):
        wait_bytes(buf2.at[:, 0, :, 0], send_b2.at[k])
        return 0

    lax.fori_loop(1, n_a, done_first_a, 0)
    lax.fori_loop(1, n_b, done_first_b, 0)
    lax.fori_loop(1, n_a2, done_second_a, 0)
    lax.fori_loop(1, n_b2, done_second_b, 0)

    @pl.when(even)
    def _():
        done_second_a(0, 0)

    @pl.when(jnp.logical_not(even))
    def _():
        done_second_b(0, 0)

    for copy in copies:
        copy.wait_send()


def local(
    n_lon,
    n_lat,
    record_values,
    record_cell,
    record_instrument,
    block_counts,
    background,
    input_weight,
    instrument_table,
    lift_weight,
    first_gain,
    attn_weight,
    mix_weight,
    second_gain,
    up_weight,
    down_weight,
):
    vmem = pl.BlockSpec(memory_space=pltpu.VMEM)
    slab = 2 * n_lon
    n_yl, n_x, n_c, n_yh, n_z = grid_of(n_lon, n_lat)
    out = pl.pallas_call(
        functools.partial(kernel, n_lon, n_lat),
        out_shape=jax.ShapeDtypeStruct((576, 192), jnp.bfloat16),
        in_specs=[pl.BlockSpec(memory_space=pltpu.HBM)] * 14,
        out_specs=vmem,
        scratch_shapes=[
            pltpu.VMEM((n_lat, 2, n_lon), jnp.int32),
            pltpu.VMEM((n_lat, 2, n_lon), jnp.int32),
            pltpu.VMEM((n_lat, n_lon), jnp.int32),
            pltpu.VMEM((288, 2, 192), jnp.bfloat16),
            pltpu.VMEM((192, 128), jnp.bfloat16),
            pltpu.VMEM((INSTR, 192), jnp.bfloat16),
            pltpu.VMEM((192, 384), jnp.bfloat16),
            pltpu.VMEM((192,), jnp.bfloat16),
            pltpu.VMEM((192, 576), jnp.bfloat16),
            pltpu.VMEM((192, 192), jnp.bfloat16),
            pltpu.VMEM((192,), jnp.bfloat16),
            pltpu.VMEM((192, 768), jnp.bfloat16),
            pltpu.VMEM((192, 768), jnp.bfloat16),
            pltpu.VMEM((TOKENS, 576), jnp.bfloat16),
            pltpu.VMEM((576, TOKENS), jnp.bfloat16),
            pltpu.SemaphoreType.DMA((13,)),
            pltpu.VMEM((n_yh, n_yl, n_c, n_x // 2, n_z, 2, 128), jnp.bfloat16),
            pltpu.VMEM((n_z, n_x, n_yl // 2, n_c, n_yh, 2, 128), jnp.bfloat16),
            pltpu.VMEM((n_yh, n_z, n_yl, n_x, n_c, 2, 128), jnp.bfloat16),
            pltpu.VMEM((n_lon, 1, 128), jnp.float32),
            pltpu.VMEM((n_lon, 1, 128), jnp.float32),
            pltpu.VMEM((n_lat, 8, 128), jnp.float32),
            pltpu.VMEM((n_lat, 8, 128), jnp.float32),
            pltpu.VMEM((CELLS, n_lat * slab), jnp.bfloat16),
            pltpu.VMEM((n_lat * slab, 512), jnp.bfloat16),
            pltpu.VMEM((TOKENS, 192), jnp.bfloat16),
            pltpu.VMEM((TOKENS, 256), jnp.bfloat16),
            pltpu.VMEM((HALO, 256), jnp.bfloat16),
            pltpu.VMEM((TOKENS, 192), jnp.bfloat16),
            pltpu.VMEM((TOKENS, 192), jnp.bfloat16),
            pltpu.VMEM((TOKENS, 192), jnp.bfloat16),
            pltpu.VMEM((HALO, 192), jnp.bfloat16),
            pltpu.VMEM((HALO, 192), jnp.bfloat16),
            pltpu.VMEM((TOKENS, 192), jnp.bfloat16),
            pltpu.VMEM((TOKENS, 192), jnp.float32),
            pltpu.SemaphoreType.DMA((2,)),
            pltpu.SemaphoreType.DMA((n_yh * n_yl * n_c,)),
            pltpu.SemaphoreType.DMA((n_x * n_z,)),
            pltpu.SemaphoreType.DMA((n_yh * n_yl * n_c // 2,)),
            pltpu.SemaphoreType.DMA((n_x * n_z // 2,)),
            pltpu.SemaphoreType.DMA,
            pltpu.SemaphoreType.DMA,
            pltpu.SemaphoreType.DMA,
            pltpu.SemaphoreType.DMA,
            pltpu.SemaphoreType.DMA,
            pltpu.SemaphoreType.DMA,
            pltpu.SemaphoreType.DMA((n_lat,)),
            pltpu.SemaphoreType.DMA((9,)),
            pltpu.SemaphoreType.DMA((9,)),
        ],
        compiler_params=pltpu.CompilerParams(
            collective_id=0, has_side_effects=True, vmem_limit_bytes=60 * 1024 * 1024
        ),
    )(
        record_values.reshape(n_yl // 2, 2, n_x // 2, 2, n_c, n_yh, n_z, 2, 128),
        record_cell.transpose(1, 2, 0),
        record_instrument.transpose(1, 2, 0),
        block_counts.transpose(1, 0),
        background.reshape(288, 2, 192),
        input_weight.T,
        instrument_table,
        lift_weight,
        first_gain,
        attn_weight,
        mix_weight,
        second_gain,
        up_weight,
        down_weight.T,
    )
    return out.reshape(12, 24, 2, 192)


def solution(mesh):
    placed = (
        P("lon", "lat", None, None),
        P("lon", "lat", None),
        P("lon", "lat", None),
        P("lon", "lat"),
        P("lat", "lon", None, None),
    ) + (P(),) * 9
    return jax.shard_map(
        functools.partial(local, mesh.shape["lon"], mesh.shape["lat"]),
        mesh=mesh,
        in_specs=placed,
        out_specs=P("lat", "lon", None, None),
        check_vma=False,
    )
```
